32 devices in a mesh: ctx: 16 (over z, y, core), ch: 2 (over x).
Axes of the slice: x: 2, y: 2, z: 4, core: 2. Of those that a mesh axis runs over, the one named last changes fastest.
Arguments:
- tokens: bfloat16 [4096, 4096], P('ctx', 'ch'), may hold values from -6 to 6
- w_in: bfloat16 [4096, 3, 4096], P('ctx', None, 'ch'), may hold values from -0.09375 to 0.09375
- taps: float32 [3, 3, 4096], P(None, None, 'ch'), may hold values from -2 to 2
- modes_gain: float32 [16, 4096], P(None, 'ch'), may hold values from -1.5 to 1.5
- decay: float32 [16, 4096], P(None, 'ch'), may hold values from 0.3 to 300
- skip: float32 [4096], P('ch'), may hold values from -4 to 4
Outputs:
- mixed: bfloat16 [4096, 4096], P('ctx', 'ch')
The draws below stay inside these ranges and needn't reach their ends.
All inputs are finite; a program needn't handle non-finite values.
Results may differ from the reference program's by a relative error of at most 0.0075.
Values may be sent and summed in bfloat16 or wider, within the bound.
A program may use at most 128 MiB of HBM per device.

```python
import math
import jax
import jax.numpy as jnp

D = 4096
MODES = 16
SEQ = 4096


def level_of(key, extent, shards, smallest, high):
    level, own = 1.0, jax.random.fold_in(key, 6)
    for axis_at, parts in shards:
        heights = jnp.exp(jax.random.uniform(jax.random.fold_in(own, axis_at), (parts,), jnp.float32, smallest / len(shards), high / len(shards)))
        level = level * jnp.repeat(heights, extent[axis_at] // parts).reshape([-1 if axis == axis_at else 1 for axis in range(len(extent))])
    return level


def normal_values(rng, shape, scale, limit, pieces=(), kind=jnp.bfloat16):
    array = scale * jax.random.normal(rng, shape, jnp.float32)
    if pieces:
        array = array * level_of(rng, shape, pieces, -0.22, 0.18)
    return jnp.clip(array, -limit, limit).astype(kind)


def setup_inputs(seed: int = 0) -> dict:
    splits = jax.random.split(jax.random.key(seed), 7)
    return {
        "tokens": normal_values(splits[0], (SEQ, D), 1.0, 6.0, ((0, 16), (1, 2))),
        "w_in": normal_values(splits[1], (D, 3, D), D ** -0.5, 0.09375, ((0, 16), (2, 2))),
        "taps": normal_values(splits[2], (3, 3, D), 0.6, 2.0, ((2, 2),), jnp.float32),
        "modes_gain": normal_values(splits[3], (MODES, D), MODES ** -0.5, 1.5, ((1, 2),), jnp.float32),
        "decay": jnp.clip(jnp.exp(math.log(300.0) - 6.9077552 * jax.random.uniform(splits[4], (MODES, D), jnp.float32) ** level_of(splits[4], (MODES, D), ((1, 2),), -0.2, 0.2)), 0.3, 300.0),
        "skip": normal_values(splits[5], (D,), 1.0, 4.0, ((0, 2),), jnp.float32),
    }


def reference(tokens, w_in, taps, modes_gain, decay, skip):
    length, width = tokens.shape
    flat = w_in.reshape(width, 3 * width)
    projected = jnp.dot(tokens, flat, preferred_element_type=jnp.float32).astype(jnp.bfloat16)
    projected = projected.reshape(length, 3, width)
    extended = jnp.concatenate([jnp.zeros((2, 3, width), jnp.bfloat16), projected], 0).astype(jnp.float32)
    features = taps[0] * extended[2:] + taps[1] * extended[1:-1] + taps[2] * extended[:-2]
    gate_out = features[:, 0]
    product = features[:, 1] * features[:, 2]
    moments = jnp.arange(length, dtype=jnp.int32).astype(jnp.float32)[:, None]
    filt = jnp.zeros((length, width), jnp.float32)
    for index in range(decay.shape[0]):
        rate = decay[index] / length
        filt = filt + modes_gain[index] * jnp.sqrt(2.0 * rate) * jnp.exp(-rate * moments)
    total = 2 * length
    spectrum = jnp.fft.rfft(product, n=total, axis=0) * jnp.fft.rfft(filt, n=total, axis=0)
    conv = jnp.fft.irfft(spectrum, n=total, axis=0)[:length]
    return (gate_out * (conv + skip * product)).astype(jnp.bfloat16)
```

```python
import functools

import jax
import jax.numpy as jnp
from jax import lax
from jax.experimental import pallas as pl
from jax.experimental.pallas import tpu as pltpu
from jax.sharding import PartitionSpec as P

SEGS = 8
LANES = 128


def flip(index, bits):
    out, bit = index, 1
    while bit <= bits:
        if bits & bit:
            out = out + bit - 2 * bit * ((index // bit) % 2)
        bit *= 2
    return out


def flip_traced(index, bits, count):
    out, bit = index, 1
    while bit < count:
        out = out + ((bits // bit) % 2) * (bit - 2 * bit * ((index // bit) % 2))
        bit *= 2
    return out


def piece_order(i, count):
    quarter = count // 4
    j = jnp.maximum(i - quarter, 0)
    turn = j % 3
    later = 2 * quarter + quarter * turn - 3 * quarter * (turn // 2) + j // 3
    return jnp.where(i < quarter, i, later)


def kernel(
    n_ctx, n_ch, groups,
    tokens, w_send, taps, gains, rates, skip, out,
    tok, w_recv, acc, prod, gate, state, ends, carry, sent, halo, halo_out,
    tok_ssem, tok_rsem, w_ssem, w_rsem, out_ssem, out_rsem, st_ssem, st_rsem, halo_sems, local_sems,
):
    rows, width = tokens.shape
    wide = w_send.shape[2] // 3
    teams = n_ctx // groups
    span = groups * rows
    seg = span // SEGS
    lane_groups = wide // LANES
    ctx, ch = lax.axis_index("ctx"), lax.axis_index("ch")
    team, place = ctx // groups, ctx % groups

    hops = [("ctx", b) for b in reversed([2**i for i in range(1, groups.bit_length() - 1)])]
    hops += [("ch", b) for b in reversed([2**i for i in range(n_ch.bit_length() - 1)])]
    hops += [("ctx", 1)]
    depth = len(hops)

    def target(hop):
        axis, bit = hop
        return (flip(ctx, bit), ch) if axis == "ctx" else (ctx, flip(ch, bit))

    def slot_of(mask):
        cbits = sum(hops[i][1] for i in range(depth) if mask >> i & 1 and hops[i][0] == "ctx")
        hbits = sum(hops[i][1] for i in range(depth) if mask >> i & 1 and hops[i][0] == "ch")
        return flip(ch, hbits) * groups + flip(place, cbits)

    barrier = pltpu.get_barrier_semaphore()

    @pl.loop(1, n_ctx)
    def _(m):
        pl.semaphore_signal(barrier, inc=1, device_id=(flip_traced(ctx, m, n_ctx), ch), device_id_type=pl.DeviceIdType.MESH)

    ch_hops = [hop for hop in hops if hop[0] == "ch"]
    for hop in ch_hops:
        pl.semaphore_signal(barrier, inc=1, device_id=target(hop), device_id_type=pl.DeviceIdType.MESH)
    own_tok = pltpu.make_async_copy(tokens, tok.at[slot_of(0)], local_sems.at[0])
    own_tok.start()
    own_w = pltpu.make_async_copy(w_send.at[place], w_recv.at[0], local_sems.at[1])
    own_w.start()
    pl.semaphore_wait(barrier, n_ctx - 1 + len(ch_hops))

    def tok_copy(mask, i):
        src = tokens if mask == 0 else tok.at[slot_of(mask)]
        return pltpu.make_async_remote_copy(
            src_ref=src,
            dst_ref=tok.at[slot_of(mask)],
            send_sem=tok_ssem.at[mask, i],
            recv_sem=tok_rsem.at[mask | 1 << i],
            device_id=target(hops[i]),
            device_id_type=pl.DeviceIdType.MESH,
        )

    def arrived(mask):
        top = mask.bit_length() - 1
        pltpu.make_async_remote_copy(
            src_ref=tok.at[slot_of(mask)],
            dst_ref=tok.at[slot_of(mask)],
            send_sem=tok_ssem.at[0, top],
            recv_sem=tok_rsem.at[mask],
            device_id=target(hops[top]),
            device_id_type=pl.DeviceIdType.MESH,
        ).wait_recv()

    for i in range(depth):
        tok_copy(0, i).start()

    def w_copy(m):
        peer = flip_traced(ctx, m, n_ctx)
        return pltpu.make_async_remote_copy(
            src_ref=w_send.at[peer % groups],
            dst_ref=w_recv.at[m],
            send_sem=w_ssem.at[m],
            recv_sem=w_rsem.at[m],
            device_id=(peer, ch),
            device_id_type=pl.DeviceIdType.MESH,
        )

    @pl.loop(1, n_ctx)
    def _(i):
        w_copy(piece_order(i, n_ctx)).start()

    acc[...] = jnp.zeros_like(acc)
    masks = sorted(range(1, 2**depth), key=lambda m: (m.bit_length() if m.bit_length() == depth else 0, bin(m).count("1"), m))
    for mask in masks:
        arrived(mask)
        for i in range(mask.bit_length(), depth):
            tok_copy(mask, i).start()
    own_tok.wait()
    own_w.wait()

    tall = 2 if groups % 2 == 0 else 1
    header = SEGS

    @pl.loop(0, n_ctx)
    def _(i):
        m = piece_order(i, n_ctx)

        @pl.when(i > 0)
        def _():
            w_copy(m).wait_recv()

        depth_rows = w_recv.shape[1]
        first = flip_traced(ctx, m, n_ctx) * depth_rows
        half, column = first // width, first % width

        @pl.loop(0, groups // tall)
        def _(part):
            left = tok[pl.ds(half * groups + part * tall, tall), :, pl.ds(pl.multiple_of(column, LANES), depth_rows)]
            left = left.reshape(tall * rows, depth_rows)
            where = pl.ds(pl.multiple_of(header + part * tall * rows, 8), tall * rows)
            acc[where, :] += jnp.dot(left, w_recv[m], preferred_element_type=jnp.float32)

    @pl.loop(0, span // 64)
    def _(part):
        where = pl.ds(pl.multiple_of(header + part * 64, 8), 64)
        acc[where, :] = acc[where, :].astype(jnp.bfloat16).astype(jnp.float32)

    halo_out[...] = acc[span : span + header, :]

    def halo_copy():
        return pltpu.make_async_remote_copy(
            src_ref=halo_out,
            dst_ref=halo,
            send_sem=halo_sems.at[0],
            recv_sem=halo_sems.at[1],
            device_id=((ctx + groups) % n_ctx, ch),
            device_id_type=pl.DeviceIdType.MESH,
        )

    @pl.when(team < teams - 1)
    def _():
        halo_copy().start()

    acc[0:header, :] = jnp.zeros((header, acc.shape[1]), jnp.float32)

    @pl.when(team > 0)
    def _():
        halo_copy().wait_recv()
        acc[0:header, :] = halo[...]

    @pl.loop(0, SEGS)
    def _(s):
        base = pl.multiple_of(s * seg, 8)
        for g in range(lane_groups):
            features = []
            for j in range(3):
                lanes = slice(j * wide + g * LANES, j * wide + (g + 1) * LANES)
                block = acc[pl.ds(base, seg + header), lanes]
                total = taps[0, j : j + 1, g * LANES : (g + 1) * LANES] * block[header:]
                total += taps[1, j : j + 1, g * LANES : (g + 1) * LANES] * pltpu.roll(block, 1, 0)[header:]
                total += taps[2, j : j + 1, g * LANES : (g + 1) * LANES] * pltpu.roll(block, 2, 0)[header:]
                features.append(total)
            gate[g, pl.ds(s, seg, stride=SEGS), :] = features[0]
            prod[g, pl.ds(s, seg, stride=SEGS), :] = features[1] * features[2]

    modes = rates.shape[0]

    def row(ref, m, g):
        return jnp.broadcast_to(ref[m : m + 1, g * LANES : (g + 1) * LANES], (SEGS, LANES))

    for g in range(lane_groups):
        keep = [jnp.exp(-row(rates, m, g)) for m in range(modes)]

        def step(t, states):
            x = prod[g, pl.ds(pl.multiple_of(t * SEGS, SEGS), SEGS), :]
            return tuple(a * s + x for a, s in zip(keep, states))

        zeros = tuple(jnp.zeros((SEGS, LANES), jnp.float32) for _ in range(modes))
        last = lax.fori_loop(0, seg, step, zeros, unroll=2)
        for m in range(modes):
            state[m, :, g * LANES : (g + 1) * LANES] = last[m]

    jump = jnp.exp(-rates[...] * float(seg))
    running = jnp.zeros_like(jump)
    for s in range(SEGS):
        ending = state[:, s, :]
        state[:, s, :] = running
        running = running * jump + ending
    ends[...] = running

    def state_copy(k):
        return pltpu.make_async_remote_copy(
            src_ref=ends,
            dst_ref=carry.at[k],
            send_sem=st_ssem.at[k],
            recv_sem=st_rsem.at[k],
            device_id=((ctx + k * groups) % n_ctx, ch),
            device_id_type=pl.DeviceIdType.MESH,
        )

    carry[0] = jnp.zeros_like(jump)
    for k in range(1, teams):
        @pl.when(team + k < teams)
        def _():
            state_copy(k).start()
    for k in range(1, teams):
        @pl.when(team >= k)
        def _():
            state_copy(k).wait_recv()
            carry[0] += carry[k] * jnp.exp(-rates[...] * float((k - 1) * span))
    incoming = carry[0]
    for s in range(SEGS):
        state[:, s, :] = state[:, s, :] + incoming * jnp.exp(-rates[...] * float(s * seg))

    for g in range(lane_groups):
        keep = [jnp.exp(-row(rates, m, g)) for m in range(modes)]
        weight = [row(gains, m, g) * jnp.sqrt(2.0 * row(rates, m, g)) for m in range(modes)]
        direct = jnp.broadcast_to(skip[0:1, g * LANES : (g + 1) * LANES], (SEGS, LANES))

        def step(t, states):
            where = pl.ds(pl.multiple_of(t * SEGS, SEGS), SEGS)
            x = prod[g, where, :]
            states = tuple(a * s + x for a, s in zip(keep, states))
            terms = [w * s for w, s in zip(weight, states)] + [direct * x]
            while len(terms) > 1:
                terms = [a + b for a, b in zip(terms[::2], terms[1::2])] + ([terms[-1]] if len(terms) % 2 else [])
            gate[g, where, :] = gate[g, where, :] * terms[0]
            return states

        start = tuple(state[m, :, g * LANES : (g + 1) * LANES] for m in range(modes))
        lax.fori_loop(0, seg, step, start)

    @pl.loop(0, SEGS)
    def _(s):
        for g in range(lane_groups):
            value = gate[g, pl.ds(s, seg, stride=SEGS), :]
            sent[pl.ds(pl.multiple_of(s * seg, 8), seg), g * LANES : (g + 1) * LANES] = value.astype(sent.dtype)

    columns = pl.ds(pl.multiple_of(place * wide, LANES), wide)

    def out_rows(p):
        return sent.at[pl.ds(pl.multiple_of(p * rows, 16), rows), :]

    def out_copy(d):
        peer = flip_traced(place, d, groups)
        return pltpu.make_async_remote_copy(
            src_ref=out_rows(peer),
            dst_ref=out.at[:, columns],
            send_sem=out_ssem.at[d],
            recv_sem=out_rsem.at[d],
            device_id=(team * groups + peer, ch),
            device_id_type=pl.DeviceIdType.MESH,
        )

    def out_arrival(d):
        peer = flip_traced(place, d, groups)
        spot = out.at[:, pl.ds(pl.multiple_of(peer * wide, LANES), wide)]
        pltpu.make_async_remote_copy(
            src_ref=spot,
            dst_ref=spot,
            send_sem=out_ssem.at[d],
            recv_sem=out_rsem.at[d],
            device_id=(team * groups + peer, ch),
            device_id_type=pl.DeviceIdType.MESH,
        ).wait_recv()

    own_out = pltpu.make_async_copy(out_rows(place), out.at[:, columns], local_sems.at[2])

    @pl.loop(1, groups)
    def _(d):
        out_copy(groups - d).start()

    own_out.start()
    for i in range(depth):
        tok_copy(0, i).wait_send()
    for mask in masks:
        for i in range(mask.bit_length(), depth):
            tok_copy(mask, i).wait_send()

    @pl.loop(1, n_ctx)
    def _(m):
        w_copy(m).wait_send()

    @pl.when(team < teams - 1)
    def _():
        halo_copy().wait_send()

    for k in range(1, teams):
        @pl.when(team + k < teams)
        def _():
            state_copy(k).wait_send()

    @pl.loop(1, groups)
    def _(d):
        out_arrival(d)
        out_copy(d).wait_send()

    own_out.wait()


def body(n_ctx, n_ch, tokens, w_in, taps, modes_gain, decay, skip):
    rows, width = tokens.shape
    e_rows, _, channels = w_in.shape
    modes = decay.shape[0]
    groups = min(n_ctx // 2, channels // LANES)
    teams = n_ctx // groups
    wide = channels // groups
    span = groups * rows
    depth = (groups * n_ch).bit_length() - 1
    place = lax.axis_index("ctx") % groups

    w_send = w_in.reshape(e_rows, 3, groups, wide).transpose(2, 0, 1, 3).reshape(groups, e_rows, 3 * wide)

    def part(array):
        return lax.dynamic_slice_in_dim(array, place * wide, wide, array.ndim - 1)

    rates = part(decay) / (rows * n_ctx)
    vmem = pl.BlockSpec(memory_space=pltpu.VMEM)
    hbm = pl.BlockSpec(memory_space=pl.ANY)
    dma = pltpu.SemaphoreType.DMA
    f32 = jnp.float32
    return pl.pallas_call(
        functools.partial(kernel, n_ctx, n_ch, groups),
        out_shape=jax.ShapeDtypeStruct((rows, channels), jnp.bfloat16),
        in_specs=[hbm, hbm, vmem, vmem, vmem, vmem],
        out_specs=hbm,
        scratch_shapes=[
            pltpu.VMEM((n_ch * groups, rows, width), tokens.dtype),
            pltpu.VMEM((n_ctx, e_rows, 3 * wide), w_in.dtype),
            pltpu.VMEM((SEGS + span, 3 * wide), f32),
            pltpu.VMEM((wide // LANES, span, LANES), f32),
            pltpu.VMEM((wide // LANES, span, LANES), f32),
            pltpu.VMEM((modes, SEGS, wide), f32),
            pltpu.VMEM((modes, wide), f32),
            pltpu.VMEM((teams, modes, wide), f32),
            pltpu.VMEM((span, wide), jnp.bfloat16),
            pltpu.VMEM((SEGS, 3 * wide), f32),
            pltpu.VMEM((SEGS, 3 * wide), f32),
            dma((2**depth, depth)),
            dma((2**depth,)),
            dma((n_ctx,)),
            dma((n_ctx,)),
            dma((groups,)),
            dma((groups,)),
            dma((teams,)),
            dma((teams,)),
            dma((2,)),
            dma((3,)),
        ],
        compiler_params=pltpu.CompilerParams(
            collective_id=0, has_side_effects=True, vmem_limit_bytes=60 * 1024 * 1024
        ),
    )(tokens, w_send, part(taps), part(modes_gain), rates, part(skip[None]))


def solution(mesh):
    in_specs = (
        P("ctx", "ch"),
        P("ctx", None, "ch"),
        P(None, None, "ch"),
        P(None, "ch"),
        P(None, "ch"),
        P("ch"),
    )
    step = functools.partial(body, mesh.shape["ctx"], mesh.shape["ch"])
    return jax.shard_map(step, mesh=mesh, in_specs=in_specs, out_specs=P("ctx", "ch"), check_vma=False)
```

```python
import functools

import jax
import jax.numpy as jnp
from jax import lax
from jax.experimental import pallas as pl
from jax.experimental.pallas import tpu as pltpu
from jax.sharding import PartitionSpec as P

SEGS = 8
LANES = 128


def flip(index, bits):
    out, bit = index, 1
    while bit <= bits:
        if bits & bit:
            out = out + bit - 2 * bit * ((index // bit) % 2)
        bit *= 2
    return out


def flip_traced(index, bits, count):
    out, bit = index, 1
    while bit < count:
        out = out + ((bits // bit) % 2) * (bit - 2 * bit * ((index // bit) % 2))
        bit *= 2
    return out


def piece_order(i, count):
    quarter = count // 4
    j = jnp.maximum(i - quarter, 0)
    turn = j % 3
    later = 2 * quarter + quarter * turn - 3 * quarter * (turn // 2) + j // 3
    return jnp.where(i < quarter, i, later)


def kernel(
    n_ctx, n_ch, groups,
    tokens, w_send, all_taps, all_gains, all_decay, all_skip, out,
    taps, gains, rates, skip, tok, w_recv, acc, prod, gate, state, ends, carry, sent, halo, halo_out,
    tok_ssem, tok_rsem, w_ssem, w_rsem, out_ssem, out_rsem, st_ssem, st_rsem, halo_sems, local_sems,
):
    rows, width = tokens.shape
    wide = w_send.shape[2] // groups
    teams = n_ctx // groups
    span = groups * rows
    seg = span // SEGS
    lane_groups = wide // LANES
    ctx, ch = lax.axis_index("ctx"), lax.axis_index("ch")
    team, place = ctx // groups, ctx % groups

    hops = [("ctx", b) for b in reversed([2**i for i in range(1, groups.bit_length() - 1)])]
    hops += [("ch", b) for b in reversed([2**i for i in range(n_ch.bit_length() - 1)])]
    hops += [("ctx", 1)]
    depth = len(hops)

    def target(hop):
        axis, bit = hop
        return (flip(ctx, bit), ch) if axis == "ctx" else (ctx, flip(ch, bit))

    def slot_of(mask):
        cbits = sum(hops[i][1] for i in range(depth) if mask >> i & 1 and hops[i][0] == "ctx")
        hbits = sum(hops[i][1] for i in range(depth) if mask >> i & 1 and hops[i][0] == "ch")
        return flip(ch, hbits) * groups + flip(place, cbits)

    barrier = pltpu.get_barrier_semaphore()

    @pl.loop(1, n_ctx)
    def _(m):
        pl.semaphore_signal(barrier, inc=1, device_id=(flip_traced(ctx, m, n_ctx), ch), device_id_type=pl.DeviceIdType.MESH)

    ch_hops = [hop for hop in hops if hop[0] == "ch"]
    for hop in ch_hops:
        pl.semaphore_signal(barrier, inc=1, device_id=target(hop), device_id_type=pl.DeviceIdType.MESH)
    own_tok = pltpu.make_async_copy(tokens, tok.at[slot_of(0)], local_sems.at[0])
    own_tok.start()

    def w_columns(p):
        return w_send.at[:, :, pl.ds(pl.multiple_of(p * wide, LANES), wide)]

    own_w = pltpu.make_async_copy(w_columns(place), w_recv.at[0], local_sems.at[1])
    own_w.start()
    own_lanes = pl.ds(pl.multiple_of(place * wide, LANES), wide)
    own_small = [
        pltpu.make_async_copy(all_taps.at[:, :, own_lanes], taps, local_sems.at[3]),
        pltpu.make_async_copy(all_gains.at[:, own_lanes], gains, local_sems.at[4]),
        pltpu.make_async_copy(all_decay.at[:, own_lanes], rates, local_sems.at[5]),
        pltpu.make_async_copy(all_skip.at[:, own_lanes], skip, local_sems.at[6]),
    ]
    for copy in own_small:
        copy.start()
    pl.semaphore_wait(barrier, n_ctx - 1 + len(ch_hops))

    def tok_copy(mask, i):
        src = tokens if mask == 0 else tok.at[slot_of(mask)]
        return pltpu.make_async_remote_copy(
            src_ref=src,
            dst_ref=tok.at[slot_of(mask)],
            send_sem=tok_ssem.at[mask, i],
            recv_sem=tok_rsem.at[mask | 1 << i],
            device_id=target(hops[i]),
            device_id_type=pl.DeviceIdType.MESH,
        )

    def arrived(mask):
        top = mask.bit_length() - 1
        pltpu.make_async_remote_copy(
            src_ref=tok.at[slot_of(mask)],
            dst_ref=tok.at[slot_of(mask)],
            send_sem=tok_ssem.at[0, top],
            recv_sem=tok_rsem.at[mask],
            device_id=target(hops[top]),
            device_id_type=pl.DeviceIdType.MESH,
        ).wait_recv()

    for i in range(depth):
        tok_copy(0, i).start()

    def w_copy(m):
        peer = flip_traced(ctx, m, n_ctx)
        return pltpu.make_async_remote_copy(
            src_ref=w_columns(peer % groups),
            dst_ref=w_recv.at[m],
            send_sem=w_ssem.at[m],
            recv_sem=w_rsem.at[m],
            device_id=(peer, ch),
            device_id_type=pl.DeviceIdType.MESH,
        )

    @pl.loop(1, n_ctx)
    def _(i):
        w_copy(piece_order(i, n_ctx)).start()

    acc[...] = jnp.zeros_like(acc)
    masks = sorted(range(1, 2**depth), key=lambda m: (m.bit_length() if m.bit_length() == depth else 0, bin(m).count("1"), m))
    for mask in masks:
        arrived(mask)
        for i in range(mask.bit_length(), depth):
            tok_copy(mask, i).start()
    own_tok.wait()
    own_w.wait()
    for copy in own_small:
        copy.wait()
    rates[...] = rates[...] / (rows * n_ctx)

    tall = 2 if groups % 2 == 0 else 1
    header = SEGS

    @pl.loop(0, n_ctx)
    def _(i):
        m = piece_order(i, n_ctx)

        @pl.when(i > 0)
        def _():
            w_copy(m).wait_recv()

        depth_rows = w_recv.shape[2]
        first = flip_traced(ctx, m, n_ctx) * depth_rows
        half, column = first // width, first % width

        @pl.loop(0, groups // tall)
        def _(part):
            left = tok[pl.ds(half * groups + part * tall, tall), :, pl.ds(pl.multiple_of(column, LANES), depth_rows)]
            left = left.reshape(tall * rows, depth_rows)
            where = pl.ds(pl.multiple_of(header + part * tall * rows, 8), tall * rows)
            for j in range(3):
                lanes = slice(j * wide, (j + 1) * wide)
                acc[where, lanes] += jnp.dot(left, w_recv[m, j], preferred_element_type=jnp.float32)

    @pl.loop(0, span // 64)
    def _(part):
        where = pl.ds(pl.multiple_of(header + part * 64, 8), 64)
        acc[where, :] = acc[where, :].astype(jnp.bfloat16).astype(jnp.float32)

    halo_out[...] = acc[span : span + header, :]

    def halo_copy():
        return pltpu.make_async_remote_copy(
            src_ref=halo_out,
            dst_ref=halo,
            send_sem=halo_sems.at[0],
            recv_sem=halo_sems.at[1],
            device_id=((ctx + groups) % n_ctx, ch),
            device_id_type=pl.DeviceIdType.MESH,
        )

    @pl.when(team < teams - 1)
    def _():
        halo_copy().start()

    acc[0:header, :] = jnp.zeros((header, acc.shape[1]), jnp.float32)

    @pl.when(team > 0)
    def _():
        halo_copy().wait_recv()
        acc[0:header, :] = halo[...]

    @pl.loop(0, SEGS)
    def _(s):
        base = pl.multiple_of(s * seg, 8)
        for g in range(lane_groups):
            features = []
            for j in range(3):
                lanes = slice(j * wide + g * LANES, j * wide + (g + 1) * LANES)
                block = acc[pl.ds(base, seg + header), lanes]
                total = taps[0, j : j + 1, g * LANES : (g + 1) * LANES] * block[header:]
                total += taps[1, j : j + 1, g * LANES : (g + 1) * LANES] * pltpu.roll(block, 1, 0)[header:]
                total += taps[2, j : j + 1, g * LANES : (g + 1) * LANES] * pltpu.roll(block, 2, 0)[header:]
                features.append(total)
            gate[g, pl.ds(s, seg, stride=SEGS), :] = features[0]
            prod[g, pl.ds(s, seg, stride=SEGS), :] = features[1] * features[2]

    modes = rates.shape[0]

    def row(ref, m, g):
        return jnp.broadcast_to(ref[m : m + 1, g * LANES : (g + 1) * LANES], (SEGS, LANES))

    for g in range(lane_groups):
        keep = [jnp.exp(-row(rates, m, g)) for m in range(modes)]

        def step(t, states):
            x = prod[g, pl.ds(pl.multiple_of(t * SEGS, SEGS), SEGS), :]
            return tuple(a * s + x for a, s in zip(keep, states))

        zeros = tuple(jnp.zeros((SEGS, LANES), jnp.float32) for _ in range(modes))
        last = lax.fori_loop(0, seg, step, zeros, unroll=2)
        for m in range(modes):
            state[m, :, g * LANES : (g + 1) * LANES] = last[m]

    jump = jnp.exp(-rates[...] * float(seg))
    running = jnp.zeros_like(jump)
    for s in range(SEGS):
        ending = state[:, s, :]
        state[:, s, :] = running
        running = running * jump + ending
    ends[...] = running

    def state_copy(k):
        return pltpu.make_async_remote_copy(
            src_ref=ends,
            dst_ref=carry.at[k],
            send_sem=st_ssem.at[k],
            recv_sem=st_rsem.at[k],
            device_id=((ctx + k * groups) % n_ctx, ch),
            device_id_type=pl.DeviceIdType.MESH,
        )

    carry[0] = jnp.zeros_like(jump)
    for k in range(1, teams):
        @pl.when(team + k < teams)
        def _():
            state_copy(k).start()
    for k in range(1, teams):
        @pl.when(team >= k)
        def _():
            state_copy(k).wait_recv()
            carry[0] += carry[k] * jnp.exp(-rates[...] * float((k - 1) * span))
    incoming = carry[0]
    for s in range(SEGS):
        state[:, s, :] = state[:, s, :] + incoming * jnp.exp(-rates[...] * float(s * seg))

    for g in range(lane_groups):
        keep = [jnp.exp(-row(rates, m, g)) for m in range(modes)]
        weight = [row(gains, m, g) * jnp.sqrt(2.0 * row(rates, m, g)) for m in range(modes)]
        direct = jnp.broadcast_to(skip[0:1, g * LANES : (g + 1) * LANES], (SEGS, LANES))

        def step(t, states):
            where = pl.ds(pl.multiple_of(t * SEGS, SEGS), SEGS)
            x = prod[g, where, :]
            states = tuple(a * s + x for a, s in zip(keep, states))
            terms = [w * s for w, s in zip(weight, states)] + [direct * x]
            while len(terms) > 1:
                terms = [a + b for a, b in zip(terms[::2], terms[1::2])] + ([terms[-1]] if len(terms) % 2 else [])
            gate[g, where, :] = gate[g, where, :] * terms[0]
            return states

        start = tuple(state[m, :, g * LANES : (g + 1) * LANES] for m in range(modes))
        lax.fori_loop(0, seg, step, start)

    @pl.loop(0, SEGS)
    def _(s):
        for g in range(lane_groups):
            value = gate[g, pl.ds(s, seg, stride=SEGS), :]
            sent[pl.ds(pl.multiple_of(s * seg, 8), seg), g * LANES : (g + 1) * LANES] = value.astype(sent.dtype)

    columns = pl.ds(pl.multiple_of(place * wide, LANES), wide)

    def out_rows(p):
        return sent.at[pl.ds(pl.multiple_of(p * rows, 16), rows), :]

    def out_copy(d):
        peer = flip_traced(place, d, groups)
        return pltpu.make_async_remote_copy(
            src_ref=out_rows(peer),
            dst_ref=out.at[:, columns],
            send_sem=out_ssem.at[d],
            recv_sem=out_rsem.at[d],
            device_id=(team * groups + peer, ch),
            device_id_type=pl.DeviceIdType.MESH,
        )

    def out_arrival(d):
        peer = flip_traced(place, d, groups)
        spot = out.at[:, pl.ds(pl.multiple_of(peer * wide, LANES), wide)]
        pltpu.make_async_remote_copy(
            src_ref=spot,
            dst_ref=spot,
            send_sem=out_ssem.at[d],
            recv_sem=out_rsem.at[d],
            device_id=(team * groups + peer, ch),
            device_id_type=pl.DeviceIdType.MESH,
        ).wait_recv()

    own_out = pltpu.make_async_copy(out_rows(place), out.at[:, columns], local_sems.at[2])

    @pl.loop(1, groups)
    def _(d):
        out_copy(groups - d).start()

    own_out.start()
    for i in range(depth):
        tok_copy(0, i).wait_send()
    for mask in masks:
        for i in range(mask.bit_length(), depth):
            tok_copy(mask, i).wait_send()

    @pl.loop(1, n_ctx)
    def _(m):
        w_copy(m).wait_send()

    @pl.when(team < teams - 1)
    def _():
        halo_copy().wait_send()

    for k in range(1, teams):
        @pl.when(team + k < teams)
        def _():
            state_copy(k).wait_send()

    @pl.loop(1, groups)
    def _(d):
        out_arrival(d)
        out_copy(d).wait_send()

    own_out.wait()


def body(n_ctx, n_ch, tokens, w_in, taps, modes_gain, decay, skip):
    rows, width = tokens.shape
    e_rows, _, channels = w_in.shape
    modes = decay.shape[0]
    groups = min(n_ctx // 2, channels // LANES)
    teams = n_ctx // groups
    wide = channels // groups
    span = groups * rows
    depth = (groups * n_ch).bit_length() - 1
    w_send = w_in.transpose(1, 0, 2)
    hbm = pl.BlockSpec(memory_space=pl.ANY)
    dma = pltpu.SemaphoreType.DMA
    f32 = jnp.float32
    return pl.pallas_call(
        functools.partial(kernel, n_ctx, n_ch, groups),
        out_shape=jax.ShapeDtypeStruct((rows, channels), jnp.bfloat16),
        in_specs=[hbm] * 6,
        out_specs=hbm,
        scratch_shapes=[
            pltpu.VMEM((3, 3, wide), f32),
            pltpu.VMEM((modes, wide), f32),
            pltpu.VMEM((modes, wide), f32),
            pltpu.VMEM((1, wide), f32),
            pltpu.VMEM((n_ch * groups, rows, width), tokens.dtype),
            pltpu.VMEM((n_ctx, 3, e_rows, wide), w_in.dtype),
            pltpu.VMEM((SEGS + span, 3 * wide), f32),
            pltpu.VMEM((wide // LANES, span, LANES), f32),
            pltpu.VMEM((wide // LANES, span, LANES), f32),
            pltpu.VMEM((modes, SEGS, wide), f32),
            pltpu.VMEM((modes, wide), f32),
            pltpu.VMEM((teams, modes, wide), f32),
            pltpu.VMEM((span, wide), jnp.bfloat16),
            pltpu.VMEM((SEGS, 3 * wide), f32),
            pltpu.VMEM((SEGS, 3 * wide), f32),
            dma((2**depth, depth)),
            dma((2**depth,)),
            dma((n_ctx,)),
            dma((n_ctx,)),
            dma((groups,)),
            dma((groups,)),
            dma((teams,)),
            dma((teams,)),
            dma((2,)),
            dma((7,)),
        ],
        compiler_params=pltpu.CompilerParams(
            collective_id=0, has_side_effects=True, vmem_limit_bytes=60 * 1024 * 1024
        ),
    )(tokens, w_send, taps, modes_gain, decay, skip[None])


def solution(mesh):
    in_specs = (
        P("ctx", "ch"),
        P("ctx", None, "ch"),
        P(None, None, "ch"),
        P(None, "ch"),
        P(None, "ch"),
        P("ch"),
    )
    step = functools.partial(body, mesh.shape["ctx"], mesh.shape["ch"])
    return jax.shard_map(step, mesh=mesh, in_specs=in_specs, out_specs=P("ctx", "ch"), check_vma=False)
```

```python
import functools

import jax
import jax.numpy as jnp
from jax import lax
from jax.experimental import pallas as pl
from jax.experimental.pallas import tpu as pltpu
from jax.sharding import PartitionSpec as P

SEGS = 8
LANES = 128


def flip(index, bits):
    out, bit = index, 1
    while bit <= bits:
        if bits & bit:
            out = out + bit - 2 * bit * ((index // bit) % 2)
        bit *= 2
    return out


def flip_traced(index, bits, count):
    out, bit = index, 1
    while bit < count:
        out = out + ((bits // bit) % 2) * (bit - 2 * bit * ((index // bit) % 2))
        bit *= 2
    return out


def piece_order(i, count):
    quarter = count // 4
    j = jnp.maximum(i - quarter, 0)
    turn = j % 3
    later = 2 * quarter + quarter * turn - 3 * quarter * (turn // 2) + j // 3
    return jnp.where(i < quarter, i, later)


def kernel(
    n_ctx, n_ch, groups,
    tokens, w_send, all_taps, all_gains, all_decay, all_skip, out,
    taps, gains, rates, skip, tok, w_recv, acc, prod, gate, state, ends, carry, sent, halo, halo_out,
    tok_ssem, tok_rsem, w_ssem, w_rsem, out_ssem, out_rsem, st_ssem, st_rsem, halo_sems, local_sems, own_sems,
):
    rows, width = tokens.shape
    wide = w_send.shape[2] // groups
    teams = n_ctx // groups
    span = groups * rows
    seg = span // SEGS
    lane_groups = wide // LANES
    ctx, ch = lax.axis_index("ctx"), lax.axis_index("ch")
    team, place = ctx // groups, ctx % groups

    hops = [("ctx", b) for b in reversed([2**i for i in range(1, groups.bit_length() - 1)])]
    hops += [("ch", b) for b in reversed([2**i for i in range(n_ch.bit_length() - 1)])]
    hops += [("ctx", 1)]
    depth = len(hops)

    def target(hop):
        axis, bit = hop
        return (flip(ctx, bit), ch) if axis == "ctx" else (ctx, flip(ch, bit))

    def slot_of(mask):
        cbits = sum(hops[i][1] for i in range(depth) if mask >> i & 1 and hops[i][0] == "ctx")
        hbits = sum(hops[i][1] for i in range(depth) if mask >> i & 1 and hops[i][0] == "ch")
        return flip(ch, hbits) * groups + flip(place, cbits)

    barrier = pltpu.get_barrier_semaphore()

    @pl.loop(1, n_ctx)
    def _(m):
        pl.semaphore_signal(barrier, inc=1, device_id=(flip_traced(ctx, m, n_ctx), ch), device_id_type=pl.DeviceIdType.MESH)

    ch_hops = [hop for hop in hops if hop[0] == "ch"]
    for hop in ch_hops:
        pl.semaphore_signal(barrier, inc=1, device_id=target(hop), device_id_type=pl.DeviceIdType.MESH)
    own_tok = pltpu.make_async_copy(tokens, tok.at[slot_of(0)], local_sems.at[0])
    own_tok.start()

    def w_columns(p, g):
        return w_send.at[:, :, pl.ds(pl.multiple_of(p * wide + g * LANES, LANES), LANES)]

    own_w = [pltpu.make_async_copy(w_columns(place, g), w_recv.at[g, 0], own_sems.at[0, g]) for g in range(lane_groups)]
    for copy in own_w:
        copy.start()
    own_lanes = pl.ds(pl.multiple_of(place * wide, LANES), wide)
    own_small = [
        pltpu.make_async_copy(all_taps.at[:, :, own_lanes], taps, local_sems.at[3]),
        pltpu.make_async_copy(all_gains.at[:, own_lanes], gains, local_sems.at[4]),
        pltpu.make_async_copy(all_decay.at[:, own_lanes], rates, local_sems.at[5]),
        pltpu.make_async_copy(all_skip.at[:, own_lanes], skip, local_sems.at[6]),
    ]
    for copy in own_small:
        copy.start()
    pl.semaphore_wait(barrier, n_ctx - 1 + len(ch_hops))

    def tok_copy(mask, i):
        src = tokens if mask == 0 else tok.at[slot_of(mask)]
        return pltpu.make_async_remote_copy(
            src_ref=src,
            dst_ref=tok.at[slot_of(mask)],
            send_sem=tok_ssem.at[mask, i],
            recv_sem=tok_rsem.at[mask | 1 << i],
            device_id=target(hops[i]),
            device_id_type=pl.DeviceIdType.MESH,
        )

    def arrived(mask):
        top = mask.bit_length() - 1
        pltpu.make_async_remote_copy(
            src_ref=tok.at[slot_of(mask)],
            dst_ref=tok.at[slot_of(mask)],
            send_sem=tok_ssem.at[0, top],
            recv_sem=tok_rsem.at[mask],
            device_id=target(hops[top]),
            device_id_type=pl.DeviceIdType.MESH,
        ).wait_recv()

    for i in range(depth):
        tok_copy(0, i).start()

    def w_copy(m, g):
        peer = flip_traced(ctx, m, n_ctx)
        return pltpu.make_async_remote_copy(
            src_ref=w_columns(peer % groups, g),
            dst_ref=w_recv.at[g, m],
            send_sem=w_ssem.at[g, m],
            recv_sem=w_rsem.at[g, m],
            device_id=(peer, ch),
            device_id_type=pl.DeviceIdType.MESH,
        )

    for g in range(lane_groups):
        @pl.loop(1, n_ctx)
        def _(i):
            w_copy(piece_order(i, n_ctx), g).start()

    acc[...] = jnp.zeros_like(acc)
    masks = sorted(range(1, 2**depth), key=lambda m: (m.bit_length() if m.bit_length() == depth else 0, bin(m).count("1"), m))
    for mask in masks:
        arrived(mask)
        for i in range(mask.bit_length(), depth):
            tok_copy(mask, i).start()
    own_tok.wait()
    for copy in own_w + own_small:
        copy.wait()
    rates[...] = rates[...] / (rows * n_ctx)

    tall = 2 if groups % 2 == 0 else 1
    header = SEGS

    modes = rates.shape[0]
    depth_rows = w_recv.shape[3]
    columns = [pl.ds(pl.multiple_of(place * wide + g * LANES, LANES), LANES) for g in range(lane_groups)]

    def project(g):
        @pl.loop(0, n_ctx)
        def _(i):
            m = piece_order(i, n_ctx)

            @pl.when(i > 0)
            def _():
                w_copy(m, g).wait_recv()

            first = flip_traced(ctx, m, n_ctx) * depth_rows
            half, column = first // width, first % width

            @pl.loop(0, groups // tall)
            def _(part):
                left = tok[pl.ds(half * groups + part * tall, tall), :, pl.ds(pl.multiple_of(column, LANES), depth_rows)]
                left = left.reshape(tall * rows, depth_rows)
                right = jnp.concatenate([w_recv[g, m, j] for j in range(3)], axis=1)
                where = pl.ds(pl.multiple_of(header + part * tall * rows, 8), tall * rows)
                acc[g, where, :] += jnp.dot(left, right, preferred_element_type=jnp.float32)

        @pl.loop(0, span // 64)
        def _(part):
            where = pl.ds(pl.multiple_of(header + part * 64, 8), 64)
            acc[g, where, :] = acc[g, where, :].astype(jnp.bfloat16).astype(jnp.float32)

    def halo_copy(g):
        return pltpu.make_async_remote_copy(
            src_ref=halo_out.at[g],
            dst_ref=halo.at[g],
            send_sem=halo_sems.at[g, 0],
            recv_sem=halo_sems.at[g, 1],
            device_id=((ctx + groups) % n_ctx, ch),
            device_id_type=pl.DeviceIdType.MESH,
        )

    def state_copy(k, g):
        return pltpu.make_async_remote_copy(
            src_ref=ends.at[g],
            dst_ref=carry.at[g, k],
            send_sem=st_ssem.at[g, k],
            recv_sem=st_rsem.at[g, k],
            device_id=((ctx + k * groups) % n_ctx, ch),
            device_id_type=pl.DeviceIdType.MESH,
        )

    def convolve(g):
        mine = slice(g * LANES, (g + 1) * LANES)
        halo_out[g] = acc[g, span : span + header, :]

        @pl.when(team < teams - 1)
        def _():
            halo_copy(g).start()

        acc[g, 0:header, :] = jnp.zeros((header, acc.shape[2]), jnp.float32)

        @pl.when(team > 0)
        def _():
            halo_copy(g).wait_recv()
            acc[g, 0:header, :] = halo[g]

        @pl.loop(0, SEGS)
        def _(s):
            base = pl.multiple_of(s * seg, 8)
            features = []
            for j in range(3):
                block = acc[g, pl.ds(base, seg + header), j * LANES : (j + 1) * LANES]
                total = taps[0, j : j + 1, mine] * block[header:]
                total += taps[1, j : j + 1, mine] * pltpu.roll(block, 1, 0)[header:]
                total += taps[2, j : j + 1, mine] * pltpu.roll(block, 2, 0)[header:]
                features.append(total)
            gate[g, pl.ds(s, seg, stride=SEGS), :] = features[0]
            prod[g, pl.ds(s, seg, stride=SEGS), :] = features[1] * features[2]

        def row(ref, m):
            return jnp.broadcast_to(ref[m : m + 1, mine], (SEGS, LANES))

        keep = [jnp.exp(-row(rates, m)) for m in range(modes)]

        def first_step(t, states):
            x = prod[g, pl.ds(pl.multiple_of(t * SEGS, SEGS), SEGS), :]
            return tuple(a * s + x for a, s in zip(keep, states))

        zeros = tuple(jnp.zeros((SEGS, LANES), jnp.float32) for _ in range(modes))
        last = lax.fori_loop(0, seg, first_step, zeros, unroll=2)
        for m in range(modes):
            state[g, m] = last[m]

        rate = rates[:, mine]
        jump = jnp.exp(-rate * float(seg))
        running = jnp.zeros_like(jump)
        for s in range(SEGS):
            ending = state[g, :, s, :]
            state[g, :, s, :] = running
            running = running * jump + ending
        ends[g] = running
        carry[g, 0] = jnp.zeros_like(jump)
        for k in range(1, teams):
            @pl.when(team + k < teams)
            def _():
                state_copy(k, g).start()
        for k in range(1, teams):
            @pl.when(team >= k)
            def _():
                state_copy(k, g).wait_recv()
                carry[g, 0] += carry[g, k] * jnp.exp(-rates[:, mine] * float((k - 1) * span))
        incoming = carry[g, 0]
        for s in range(SEGS):
            state[g, :, s, :] = state[g, :, s, :] + incoming * jnp.exp(-rate * float(s * seg))

        weight = [row(gains, m) * jnp.sqrt(2.0 * row(rates, m)) for m in range(modes)]
        direct = jnp.broadcast_to(skip[0:1, mine], (SEGS, LANES))

        def second_step(t, states):
            where = pl.ds(pl.multiple_of(t * SEGS, SEGS), SEGS)
            x = prod[g, where, :]
            states = tuple(a * s + x for a, s in zip(keep, states))
            terms = [w * s for w, s in zip(weight, states)] + [direct * x]
            while len(terms) > 1:
                terms = [a + b for a, b in zip(terms[::2], terms[1::2])] + ([terms[-1]] if len(terms) % 2 else [])
            gate[g, where, :] = gate[g, where, :] * terms[0]
            return states

        lax.fori_loop(0, seg, second_step, tuple(state[g, m] for m in range(modes)))

        @pl.loop(0, SEGS)
        def _(s):
            value = gate[g, pl.ds(s, seg, stride=SEGS), :]
            sent[g, pl.ds(pl.multiple_of(s * seg, 8), seg), :] = value.astype(sent.dtype)

    def out_rows(p, g):
        return sent.at[g, pl.ds(pl.multiple_of(p * rows, 16), rows), :]

    def out_copy(d, g):
        peer = flip_traced(place, d, groups)
        return pltpu.make_async_remote_copy(
            src_ref=out_rows(peer, g),
            dst_ref=out.at[:, columns[g]],
            send_sem=out_ssem.at[g, d],
            recv_sem=out_rsem.at[g, d],
            device_id=(team * groups + peer, ch),
            device_id_type=pl.DeviceIdType.MESH,
        )

    def out_arrival(d, g):
        peer = flip_traced(place, d, groups)
        spot = out.at[:, pl.ds(pl.multiple_of(peer * wide + g * LANES, LANES), LANES)]
        return pltpu.make_async_remote_copy(
            src_ref=spot,
            dst_ref=spot,
            send_sem=out_ssem.at[g, d],
            recv_sem=out_rsem.at[g, d],
            device_id=(team * groups + peer, ch),
            device_id_type=pl.DeviceIdType.MESH,
        )

    own_out = [pltpu.make_async_copy(out_rows(place, g), out.at[:, columns[g]], own_sems.at[1, g]) for g in range(lane_groups)]
    for g in range(lane_groups):
        project(g)
        convolve(g)

        @pl.loop(1, groups)
        def _(d):
            out_copy(groups - d, g).start()

        own_out[g].start()

    for i in range(depth):
        tok_copy(0, i).wait_send()
    for mask in masks:
        for i in range(mask.bit_length(), depth):
            tok_copy(mask, i).wait_send()

    for g in range(lane_groups):
        @pl.loop(1, n_ctx)
        def _(m):
            w_copy(m, g).wait_send()

        @pl.when(team < teams - 1)
        def _():
            halo_copy(g).wait_send()

        for k in range(1, teams):
            @pl.when(team + k < teams)
            def _():
                state_copy(k, g).wait_send()

        @pl.loop(1, groups)
        def _(d):
            out_arrival(d, g).wait_recv()
            out_copy(d, g).wait_send()

        own_out[g].wait()


def body(n_ctx, n_ch, tokens, w_in, taps, modes_gain, decay, skip):
    rows, width = tokens.shape
    e_rows, _, channels = w_in.shape
    modes = decay.shape[0]
    groups = min(n_ctx // 2, channels // LANES)
    teams = n_ctx // groups
    wide = channels // groups
    span = groups * rows
    parts = wide // LANES
    depth = (groups * n_ch).bit_length() - 1
    w_send = w_in.transpose(1, 0, 2)
    hbm = pl.BlockSpec(memory_space=pl.ANY)
    dma = pltpu.SemaphoreType.DMA
    f32 = jnp.float32
    return pl.pallas_call(
        functools.partial(kernel, n_ctx, n_ch, groups),
        out_shape=jax.ShapeDtypeStruct((rows, channels), jnp.bfloat16),
        in_specs=[hbm] * 6,
        out_specs=hbm,
        scratch_shapes=[
            pltpu.VMEM((3, 3, wide), f32),
            pltpu.VMEM((modes, wide), f32),
            pltpu.VMEM((modes, wide), f32),
            pltpu.VMEM((1, wide), f32),
            pltpu.VMEM((n_ch * groups, rows, width), tokens.dtype),
            pltpu.VMEM((parts, n_ctx, 3, e_rows, LANES), w_in.dtype),
            pltpu.VMEM((parts, SEGS + span, 3 * LANES), f32),
            pltpu.VMEM((parts, span, LANES), f32),
            pltpu.VMEM((parts, span, LANES), f32),
            pltpu.VMEM((parts, modes, SEGS, LANES), f32),
            pltpu.VMEM((parts, modes, LANES), f32),
            pltpu.VMEM((parts, teams, modes, LANES), f32),
            pltpu.VMEM((parts, span, LANES), jnp.bfloat16),
            pltpu.VMEM((parts, SEGS, 3 * LANES), f32),
            pltpu.VMEM((parts, SEGS, 3 * LANES), f32),
            dma((2**depth, depth)),
            dma((2**depth,)),
            dma((parts, n_ctx)),
            dma((parts, n_ctx)),
            dma((parts, groups)),
            dma((parts, groups)),
            dma((parts, teams)),
            dma((parts, teams)),
            dma((parts, 2)),
            dma((7,)),
            dma((2, parts)),
        ],
        compiler_params=pltpu.CompilerParams(
            collective_id=0, has_side_effects=True, vmem_limit_bytes=60 * 1024 * 1024
        ),
    )(tokens, w_send, taps, modes_gain, decay, skip[None])


def solution(mesh):
    in_specs = (
        P("ctx", "ch"),
        P("ctx", None, "ch"),
        P(None, None, "ch"),
        P(None, "ch"),
        P(None, "ch"),
        P("ch"),
    )
    step = functools.partial(body, mesh.shape["ctx"], mesh.shape["ch"])
    return jax.shard_map(step, mesh=mesh, in_specs=in_specs, out_specs=P("ctx", "ch"), check_vma=False)
```

```python
import functools

import jax
import jax.numpy as jnp
from jax import lax
from jax.experimental import pallas as pl
from jax.experimental.pallas import tpu as pltpu
from jax.sharding import PartitionSpec as P

SEGS = 8
LANES = 128


def flip(index, bits):
    out, bit = index, 1
    while bit <= bits:
        if bits & bit:
            out = out + bit - 2 * bit * ((index // bit) % 2)
        bit *= 2
    return out


def flip_traced(index, bits, count):
    out, bit = index, 1
    while bit < count:
        out = out + ((bits // bit) % 2) * (bit - 2 * bit * ((index // bit) % 2))
        bit *= 2
    return out


def piece_order(i, count):
    quarter = count // 4
    j = jnp.maximum(i - quarter, 0)
    turn = j % 3
    later = quarter + quarter * turn + j // 3
    return jnp.where(i < quarter, i, later)


def kernel(
    n_ctx, n_ch, groups,
    tokens, w_send, all_taps, all_gains, all_decay, all_skip, out,
    taps, gains, rates, skip, tok, w_recv, acc, prod, gate, state, ends, carry, sent, halo, halo_out,
    tok_ssem, tok_rsem, w_ssem, w_rsem, out_ssem, out_rsem, st_ssem, st_rsem, halo_sems, local_sems, own_sems,
):
    rows, width = tokens.shape
    wide = w_send.shape[2] // groups
    teams = n_ctx // groups
    span = groups * rows
    seg = span // SEGS
    lane_groups = wide // LANES
    ctx, ch = lax.axis_index("ctx"), lax.axis_index("ch")
    team, place = ctx // groups, ctx % groups

    hops = [("ctx", b) for b in reversed([2**i for i in range(1, groups.bit_length() - 1)])]
    hops += [("ch", b) for b in reversed([2**i for i in range(n_ch.bit_length() - 1)])]
    hops += [("ctx", 1)]
    depth = len(hops)

    def target(hop):
        axis, bit = hop
        return (flip(ctx, bit), ch) if axis == "ctx" else (ctx, flip(ch, bit))

    def slot_of(mask):
        cbits = sum(hops[i][1] for i in range(depth) if mask >> i & 1 and hops[i][0] == "ctx")
        hbits = sum(hops[i][1] for i in range(depth) if mask >> i & 1 and hops[i][0] == "ch")
        return flip(ch, hbits) * groups + flip(place, cbits)

    barrier = pltpu.get_barrier_semaphore()

    @pl.loop(1, n_ctx)
    def _(m):
        pl.semaphore_signal(barrier, inc=1, device_id=(flip_traced(ctx, m, n_ctx), ch), device_id_type=pl.DeviceIdType.MESH)

    ch_hops = [hop for hop in hops if hop[0] == "ch"]
    for hop in ch_hops:
        pl.semaphore_signal(barrier, inc=1, device_id=target(hop), device_id_type=pl.DeviceIdType.MESH)
    own_tok = pltpu.make_async_copy(tokens, tok.at[slot_of(0)], local_sems.at[0])
    own_tok.start()

    def w_columns(p, g):
        return w_send.at[:, :, pl.ds(pl.multiple_of(p * wide + g * LANES, LANES), LANES)]

    own_w = [pltpu.make_async_copy(w_columns(place, g), w_recv.at[g, 0], own_sems.at[0, g]) for g in range(lane_groups)]
    for copy in own_w:
        copy.start()
    own_lanes = pl.ds(pl.multiple_of(place * wide, LANES), wide)
    own_small = [
        pltpu.make_async_copy(all_taps.at[:, :, own_lanes], taps, local_sems.at[3]),
        pltpu.make_async_copy(all_gains.at[:, own_lanes], gains, local_sems.at[4]),
        pltpu.make_async_copy(all_decay.at[:, own_lanes], rates, local_sems.at[5]),
        pltpu.make_async_copy(all_skip.at[:, own_lanes], skip, local_sems.at[6]),
    ]
    for copy in own_small:
        copy.start()
    pl.semaphore_wait(barrier, n_ctx - 1 + len(ch_hops))

    def tok_copy(mask, i):
        src = tokens if mask == 0 else tok.at[slot_of(mask)]
        return pltpu.make_async_remote_copy(
            src_ref=src,
            dst_ref=tok.at[slot_of(mask)],
            send_sem=tok_ssem.at[mask, i],
            recv_sem=tok_rsem.at[mask | 1 << i],
            device_id=target(hops[i]),
            device_id_type=pl.DeviceIdType.MESH,
        )

    def arrived(mask):
        top = mask.bit_length() - 1
        pltpu.make_async_remote_copy(
            src_ref=tok.at[slot_of(mask)],
            dst_ref=tok.at[slot_of(mask)],
            send_sem=tok_ssem.at[0, top],
            recv_sem=tok_rsem.at[mask],
            device_id=target(hops[top]),
            device_id_type=pl.DeviceIdType.MESH,
        ).wait_recv()

    for i in range(depth):
        tok_copy(0, i).start()

    def w_copy(m, g):
        peer = flip_traced(ctx, m, n_ctx)
        return pltpu.make_async_remote_copy(
            src_ref=w_columns(peer % groups, g),
            dst_ref=w_recv.at[g, m],
            send_sem=w_ssem.at[g, m],
            recv_sem=w_rsem.at[g, m],
            device_id=(peer, ch),
            device_id_type=pl.DeviceIdType.MESH,
        )

    for g in range(lane_groups):
        @pl.loop(1, n_ctx)
        def _(i):
            w_copy(2 * piece_order(i // 2, n_ctx // 2) + i % 2, g).start()

    acc[...] = jnp.zeros_like(acc)
    masks = sorted(range(1, 2**depth), key=lambda m: (m.bit_length() if m.bit_length() == depth else 0, bin(m).count("1"), m))
    for mask in masks:
        arrived(mask)
        for i in range(mask.bit_length(), depth):
            tok_copy(mask, i).start()
    own_tok.wait()
    for copy in own_w + own_small:
        copy.wait()
    rates[...] = rates[...] / (rows * n_ctx)

    tall = 4 if groups % 4 == 0 else 1
    header = SEGS

    modes = rates.shape[0]
    depth_rows = w_recv.shape[3]
    columns = [pl.ds(pl.multiple_of(place * wide + g * LANES, LANES), LANES) for g in range(lane_groups)]

    def project(g):
        @pl.loop(0, n_ctx // 2)
        def _(i):
            m = 2 * piece_order(i, n_ctx // 2)
            odd = ctx % 2

            @pl.when(i > 0)
            def _():
                w_copy(m, g).wait_recv()

            w_copy(m + 1, g).wait_recv()
            first = flip_traced(ctx - odd, m, n_ctx) * depth_rows
            half, column = first // width, first % width

            @pl.loop(0, groups // tall)
            def _(part):
                left = tok[pl.ds(half * groups + part * tall, tall), :, pl.ds(pl.multiple_of(column, LANES), 2 * depth_rows)]
                left = left.reshape(tall * rows, 2 * depth_rows)
                pair = (m + odd, m + 1 - odd)
                right = jnp.concatenate(
                    [jnp.concatenate([w_recv[g, p, j] for p in pair], axis=0) for j in range(3)], axis=1
                )
                where = pl.ds(pl.multiple_of(header + part * tall * rows, 8), tall * rows)
                acc[g, where, :] += jnp.dot(left, right, preferred_element_type=jnp.float32)

        @pl.loop(0, span // 64)
        def _(part):
            where = pl.ds(pl.multiple_of(header + part * 64, 8), 64)
            acc[g, where, :] = acc[g, where, :].astype(jnp.bfloat16).astype(jnp.float32)

    def halo_copy(g):
        return pltpu.make_async_remote_copy(
            src_ref=halo_out.at[g],
            dst_ref=halo.at[g],
            send_sem=halo_sems.at[g, 0],
            recv_sem=halo_sems.at[g, 1],
            device_id=((ctx + groups) % n_ctx, ch),
            device_id_type=pl.DeviceIdType.MESH,
        )

    def state_copy(k, g):
        return pltpu.make_async_remote_copy(
            src_ref=ends.at[g],
            dst_ref=carry.at[g, k],
            send_sem=st_ssem.at[g, k],
            recv_sem=st_rsem.at[g, k],
            device_id=((ctx + k * groups) % n_ctx, ch),
            device_id_type=pl.DeviceIdType.MESH,
        )

    def convolve(g):
        mine = slice(g * LANES, (g + 1) * LANES)
        halo_out[g] = acc[g, span : span + header, :]

        @pl.when(team < teams - 1)
        def _():
            halo_copy(g).start()

        acc[g, 0:header, :] = jnp.zeros((header, acc.shape[2]), jnp.float32)

        @pl.when(team > 0)
        def _():
            halo_copy(g).wait_recv()
            acc[g, 0:header, :] = halo[g]

        @pl.loop(0, SEGS)
        def _(s):
            base = pl.multiple_of(s * seg, 8)
            features = []
            for j in range(3):
                block = acc[g, pl.ds(base, seg + header), j * LANES : (j + 1) * LANES]
                total = taps[0, j : j + 1, mine] * block[header:]
                total += taps[1, j : j + 1, mine] * pltpu.roll(block, 1, 0)[header:]
                total += taps[2, j : j + 1, mine] * pltpu.roll(block, 2, 0)[header:]
                features.append(total)
            gate[g, pl.ds(s, seg, stride=SEGS), :] = features[0]
            prod[g, pl.ds(s, seg, stride=SEGS), :] = features[1] * features[2]

        def row(ref, m):
            return jnp.broadcast_to(ref[m : m + 1, mine], (SEGS, LANES))

        keep = [jnp.exp(-row(rates, m)) for m in range(modes)]

        def first_step(t, states):
            x = prod[g, pl.ds(pl.multiple_of(t * SEGS, SEGS), SEGS), :]
            return tuple(a * s + x for a, s in zip(keep, states))

        zeros = tuple(jnp.zeros((SEGS, LANES), jnp.float32) for _ in range(modes))
        last = lax.fori_loop(0, seg, first_step, zeros, unroll=2)
        for m in range(modes):
            state[g, m] = last[m]

        rate = rates[:, mine]
        jump = jnp.exp(-rate * float(seg))
        running = jnp.zeros_like(jump)
        for s in range(SEGS):
            ending = state[g, :, s, :]
            state[g, :, s, :] = running
            running = running * jump + ending
        ends[g] = running
        carry[g, 0] = jnp.zeros_like(jump)
        for k in range(1, teams):
            @pl.when(team + k < teams)
            def _():
                state_copy(k, g).start()
        for k in range(1, teams):
            @pl.when(team >= k)
            def _():
                state_copy(k, g).wait_recv()
                carry[g, 0] += carry[g, k] * jnp.exp(-rates[:, mine] * float((k - 1) * span))
        incoming = carry[g, 0]
        for s in range(SEGS):
            state[g, :, s, :] = state[g, :, s, :] + incoming * jnp.exp(-rate * float(s * seg))

        weight = [row(gains, m) * jnp.sqrt(2.0 * row(rates, m)) for m in range(modes)]
        direct = jnp.broadcast_to(skip[0:1, mine], (SEGS, LANES))

        def second_step(t, states):
            where = pl.ds(pl.multiple_of(t * SEGS, SEGS), SEGS)
            x = prod[g, where, :]
            states = tuple(a * s + x for a, s in zip(keep, states))
            terms = [w * s for w, s in zip(weight, states)] + [direct * x]
            while len(terms) > 1:
                terms = [a + b for a, b in zip(terms[::2], terms[1::2])] + ([terms[-1]] if len(terms) % 2 else [])
            gate[g, where, :] = gate[g, where, :] * terms[0]
            return states

        lax.fori_loop(0, seg, second_step, tuple(state[g, m] for m in range(modes)))

        @pl.loop(0, SEGS)
        def _(s):
            value = gate[g, pl.ds(s, seg, stride=SEGS), :]
            sent[g, pl.ds(pl.multiple_of(s * seg, 8), seg), :] = value.astype(sent.dtype)

    def out_rows(p, g):
        return sent.at[g, pl.ds(pl.multiple_of(p * rows, 16), rows), :]

    def out_copy(d, g):
        peer = flip_traced(place, d, groups)
        return pltpu.make_async_remote_copy(
            src_ref=out_rows(peer, g),
            dst_ref=out.at[:, columns[g]],
            send_sem=out_ssem.at[g, d],
            recv_sem=out_rsem.at[g, d],
            device_id=(team * groups + peer, ch),
            device_id_type=pl.DeviceIdType.MESH,
        )

    def out_arrival(d, g):
        peer = flip_traced(place, d, groups)
        spot = out.at[:, pl.ds(pl.multiple_of(peer * wide + g * LANES, LANES), LANES)]
        return pltpu.make_async_remote_copy(
            src_ref=spot,
            dst_ref=spot,
            send_sem=out_ssem.at[g, d],
            recv_sem=out_rsem.at[g, d],
            device_id=(team * groups + peer, ch),
            device_id_type=pl.DeviceIdType.MESH,
        )

    own_out = [pltpu.make_async_copy(out_rows(place, g), out.at[:, columns[g]], own_sems.at[1, g]) for g in range(lane_groups)]
    for g in range(lane_groups):
        project(g)
        convolve(g)

        @pl.loop(1, groups)
        def _(d):
            out_copy(groups - d, g).start()

        own_out[g].start()

    for i in range(depth):
        tok_copy(0, i).wait_send()
    for mask in masks:
        for i in range(mask.bit_length(), depth):
            tok_copy(mask, i).wait_send()

    for g in range(lane_groups):
        @pl.loop(1, n_ctx)
        def _(m):
            w_copy(m, g).wait_send()

        @pl.when(team < teams - 1)
        def _():
            halo_copy(g).wait_send()

        for k in range(1, teams):
            @pl.when(team + k < teams)
            def _():
                state_copy(k, g).wait_send()

        @pl.loop(1, groups)
        def _(d):
            out_arrival(d, g).wait_recv()
            out_copy(d, g).wait_send()

        own_out[g].wait()


def body(n_ctx, n_ch, tokens, w_in, taps, modes_gain, decay, skip):
    rows, width = tokens.shape
    e_rows, _, channels = w_in.shape
    modes = decay.shape[0]
    groups = min(n_ctx // 2, channels // LANES)
    teams = n_ctx // groups
    wide = channels // groups
    span = groups * rows
    parts = wide // LANES
    depth = (groups * n_ch).bit_length() - 1
    w_send = w_in.transpose(1, 0, 2)
    hbm = pl.BlockSpec(memory_space=pl.ANY)
    dma = pltpu.SemaphoreType.DMA
    f32 = jnp.float32
    return pl.pallas_call(
        functools.partial(kernel, n_ctx, n_ch, groups),
        out_shape=jax.ShapeDtypeStruct((rows, channels), jnp.bfloat16),
        in_specs=[hbm] * 6,
        out_specs=hbm,
        scratch_shapes=[
            pltpu.VMEM((3, 3, wide), f32),
            pltpu.VMEM((modes, wide), f32),
            pltpu.VMEM((modes, wide), f32),
            pltpu.VMEM((1, wide), f32),
            pltpu.VMEM((n_ch * groups, rows, width), tokens.dtype),
            pltpu.VMEM((parts, n_ctx, 3, e_rows, LANES), w_in.dtype),
            pltpu.VMEM((parts, SEGS + span, 3 * LANES), f32),
            pltpu.VMEM((parts, span, LANES), f32),
            pltpu.VMEM((parts, span, LANES), f32),
            pltpu.VMEM((parts, modes, SEGS, LANES), f32),
            pltpu.VMEM((parts, modes, LANES), f32),
            pltpu.VMEM((parts, teams, modes, LANES), f32),
            pltpu.VMEM((parts, span, LANES), jnp.bfloat16),
            pltpu.VMEM((parts, SEGS, 3 * LANES), f32),
            pltpu.VMEM((parts, SEGS, 3 * LANES), f32),
            dma((2**depth, depth)),
            dma((2**depth,)),
            dma((parts, n_ctx)),
            dma((parts, n_ctx)),
            dma((parts, groups)),
            dma((parts, groups)),
            dma((parts, teams)),
            dma((parts, teams)),
            dma((parts, 2)),
            dma((7,)),
            dma((2, parts)),
        ],
        compiler_params=pltpu.CompilerParams(
            collective_id=0, has_side_effects=True, vmem_limit_bytes=60 * 1024 * 1024
        ),
    )(tokens, w_send, taps, modes_gain, decay, skip[None])


def solution(mesh):
    in_specs = (
        P("ctx", "ch"),
        P("ctx", None, "ch"),
        P(None, None, "ch"),
        P(None, "ch"),
        P(None, "ch"),
        P("ch"),
    )
    step = functools.partial(body, mesh.shape["ctx"], mesh.shape["ch"])
    return jax.shard_map(step, mesh=mesh, in_specs=in_specs, out_specs=P("ctx", "ch"), check_vma=False)
```

```python
import functools

import jax
import jax.numpy as jnp
from jax import lax
from jax.experimental import pallas as pl
from jax.experimental.pallas import tpu as pltpu
from jax.sharding import PartitionSpec as P

SEGS = 8
LANES = 128


def flip(index, bits):
    out, bit = index, 1
    while bit <= bits:
        if bits & bit:
            out = out + bit - 2 * bit * ((index // bit) % 2)
        bit *= 2
    return out


def flip_traced(index, bits, count):
    out, bit = index, 1
    while bit < count:
        out = out + ((bits // bit) % 2) * (bit - 2 * bit * ((index // bit) % 2))
        bit *= 2
    return out


def piece_order(i, count):
    quarter = count // 4
    j = jnp.maximum(i - quarter, 0)
    turn = j % 3
    later = quarter + quarter * turn + j // 3
    return jnp.where(i < quarter, i, later)


def kernel(
    n_ctx, n_ch, groups,
    tokens, w_send, all_taps, all_gains, all_decay, all_skip, out,
    taps, gains, rates, skip, tok, w_recv, acc, prod, gate, state, ends, carry, sent, halo, halo_out,
    tok_ssem, tok_rsem, w_ssem, w_rsem, out_ssem, out_rsem, st_ssem, st_rsem, halo_sems, local_sems, own_sems,
):
    rows, width = tokens.shape
    wide = w_send.shape[2] // groups
    teams = n_ctx // groups
    span = groups * rows
    seg = span // SEGS
    lane_groups = wide // LANES
    ctx, ch = lax.axis_index("ctx"), lax.axis_index("ch")
    team, place = ctx // groups, ctx % groups

    hops = [("ctx", b) for b in reversed([2**i for i in range(1, groups.bit_length() - 1)])]
    hops += [("ch", b) for b in reversed([2**i for i in range(n_ch.bit_length() - 1)])]
    hops += [("ctx", 1)]
    depth = len(hops)

    def target(hop):
        axis, bit = hop
        return (flip(ctx, bit), ch) if axis == "ctx" else (ctx, flip(ch, bit))

    def slot_of(mask):
        cbits = sum(hops[i][1] for i in range(depth) if mask >> i & 1 and hops[i][0] == "ctx")
        hbits = sum(hops[i][1] for i in range(depth) if mask >> i & 1 and hops[i][0] == "ch")
        return flip(ch, hbits) * groups + flip(place, cbits)

    barrier = pltpu.get_barrier_semaphore()

    @pl.loop(1, n_ctx)
    def _(m):
        pl.semaphore_signal(barrier, inc=1, device_id=(flip_traced(ctx, m, n_ctx), ch), device_id_type=pl.DeviceIdType.MESH)

    ch_hops = [hop for hop in hops if hop[0] == "ch"]
    for hop in ch_hops:
        pl.semaphore_signal(barrier, inc=1, device_id=target(hop), device_id_type=pl.DeviceIdType.MESH)
    own_tok = pltpu.make_async_copy(tokens, tok.at[slot_of(0)], local_sems.at[0])
    own_tok.start()

    def w_columns(p, g):
        return w_send.at[:, :, pl.ds(pl.multiple_of(p * wide + g * LANES, LANES), LANES)]

    own_w = [pltpu.make_async_copy(w_columns(place, g), w_recv.at[g, 0], own_sems.at[0, g]) for g in range(lane_groups)]
    for copy in own_w:
        copy.start()
    own_lanes = pl.ds(pl.multiple_of(place * wide, LANES), wide)
    own_small = [
        pltpu.make_async_copy(all_taps.at[:, :, own_lanes], taps, local_sems.at[3]),
        pltpu.make_async_copy(all_gains.at[:, own_lanes], gains, local_sems.at[4]),
        pltpu.make_async_copy(all_decay.at[:, own_lanes], rates, local_sems.at[5]),
        pltpu.make_async_copy(all_skip.at[:, own_lanes], skip, local_sems.at[6]),
    ]
    for copy in own_small:
        copy.start()
    pl.semaphore_wait(barrier, n_ctx - 1 + len(ch_hops))

    def tok_copy(mask, i):
        src = tokens if mask == 0 else tok.at[slot_of(mask)]
        return pltpu.make_async_remote_copy(
            src_ref=src,
            dst_ref=tok.at[slot_of(mask)],
            send_sem=tok_ssem.at[mask, i],
            recv_sem=tok_rsem.at[mask | 1 << i],
            device_id=target(hops[i]),
            device_id_type=pl.DeviceIdType.MESH,
        )

    def arrived(mask):
        top = mask.bit_length() - 1
        pltpu.make_async_remote_copy(
            src_ref=tok.at[slot_of(mask)],
            dst_ref=tok.at[slot_of(mask)],
            send_sem=tok_ssem.at[0, top],
            recv_sem=tok_rsem.at[mask],
            device_id=target(hops[top]),
            device_id_type=pl.DeviceIdType.MESH,
        ).wait_recv()

    for i in range(depth):
        tok_copy(0, i).start()

    def w_copy(m, g):
        peer = flip_traced(ctx, m, n_ctx)
        return pltpu.make_async_remote_copy(
            src_ref=w_columns(peer % groups, g),
            dst_ref=w_recv.at[g, m],
            send_sem=w_ssem.at[g, m],
            recv_sem=w_rsem.at[g, m],
            device_id=(peer, ch),
            device_id_type=pl.DeviceIdType.MESH,
        )

    for g in range(lane_groups):
        @pl.loop(1, n_ctx)
        def _(i):
            w_copy(2 * piece_order(i // 2, n_ctx // 2) + i % 2, g).start()

    acc[...] = jnp.zeros_like(acc)
    masks = sorted(range(1, 2**depth), key=lambda m: (m.bit_length() if m.bit_length() == depth else 0, bin(m).count("1"), m))
    for mask in masks:
        arrived(mask)
        for i in range(mask.bit_length(), depth):
            tok_copy(mask, i).start()
    own_tok.wait()
    for copy in own_w + own_small:
        copy.wait()
    rates[...] = rates[...] / (rows * n_ctx)

    tall = groups
    header = SEGS

    modes = rates.shape[0]
    depth_rows = w_recv.shape[3]
    columns = [pl.ds(pl.multiple_of(place * wide + g * LANES, LANES), LANES) for g in range(lane_groups)]

    def project(g):
        @pl.loop(0, n_ctx // 2)
        def _(i):
            m = 2 * piece_order(i, n_ctx // 2)
            odd = ctx % 2

            @pl.when(i > 0)
            def _():
                w_copy(m, g).wait_recv()

            w_copy(m + 1, g).wait_recv()
            first = flip_traced(ctx - odd, m, n_ctx) * depth_rows
            half, column = first // width, first % width

            @pl.loop(0, groups // tall)
            def _(part):
                left = tok[pl.ds(half * groups + part * tall, tall), :, pl.ds(pl.multiple_of(column, LANES), 2 * depth_rows)]
                left = left.reshape(tall * rows, 2 * depth_rows)
                pair = (m + odd, m + 1 - odd)
                right = jnp.concatenate(
                    [jnp.concatenate([w_recv[g, p, j] for p in pair], axis=0) for j in range(3)], axis=1
                )
                where = pl.ds(pl.multiple_of(header + part * tall * rows, 8), tall * rows)
                acc[g, where, :] += jnp.dot(left, right, preferred_element_type=jnp.float32)

        @pl.loop(0, span // 64)
        def _(part):
            where = pl.ds(pl.multiple_of(header + part * 64, 8), 64)
            acc[g, where, :] = acc[g, where, :].astype(jnp.bfloat16).astype(jnp.float32)

    def halo_copy(g):
        return pltpu.make_async_remote_copy(
            src_ref=halo_out.at[g],
            dst_ref=halo.at[g],
            send_sem=halo_sems.at[g, 0],
            recv_sem=halo_sems.at[g, 1],
            device_id=((ctx + groups) % n_ctx, ch),
            device_id_type=pl.DeviceIdType.MESH,
        )

    def state_copy(k, g):
        return pltpu.make_async_remote_copy(
            src_ref=ends.at[g],
            dst_ref=carry.at[g, k],
            send_sem=st_ssem.at[g, k],
            recv_sem=st_rsem.at[g, k],
            device_id=((ctx + k * groups) % n_ctx, ch),
            device_id_type=pl.DeviceIdType.MESH,
        )

    def convolve(g):
        mine = slice(g * LANES, (g + 1) * LANES)
        halo_out[g] = acc[g, span : span + header, :]

        @pl.when(team < teams - 1)
        def _():
            halo_copy(g).start()

        acc[g, 0:header, :] = jnp.zeros((header, acc.shape[2]), jnp.float32)

        @pl.when(team > 0)
        def _():
            halo_copy(g).wait_recv()
            acc[g, 0:header, :] = halo[g]

        @pl.loop(0, SEGS)
        def _(s):
            base = pl.multiple_of(s * seg, 8)
            features = []
            for j in range(3):
                block = acc[g, pl.ds(base, seg + header), j * LANES : (j + 1) * LANES]
                total = taps[0, j : j + 1, mine] * block[header:]
                total += taps[1, j : j + 1, mine] * pltpu.roll(block, 1, 0)[header:]
                total += taps[2, j : j + 1, mine] * pltpu.roll(block, 2, 0)[header:]
                features.append(total)
            gate[g, pl.ds(s, seg, stride=SEGS), :] = features[0]
            prod[g, pl.ds(s, seg, stride=SEGS), :] = features[1] * features[2]

        def row(ref, m):
            return jnp.broadcast_to(ref[m : m + 1, mine], (SEGS, LANES))

        keep = [jnp.exp(-row(rates, m)) for m in range(modes)]

        def first_step(t, states):
            x = prod[g, pl.ds(pl.multiple_of(t * SEGS, SEGS), SEGS), :]
            return tuple(a * s + x for a, s in zip(keep, states))

        zeros = tuple(jnp.zeros((SEGS, LANES), jnp.float32) for _ in range(modes))
        last = lax.fori_loop(0, seg, first_step, zeros, unroll=2)
        for m in range(modes):
            state[g, m] = last[m]

        rate = rates[:, mine]
        jump = jnp.exp(-rate * float(seg))
        running = jnp.zeros_like(jump)
        for s in range(SEGS):
            ending = state[g, :, s, :]
            state[g, :, s, :] = running
            running = running * jump + ending
        ends[g] = running
        carry[g, 0] = jnp.zeros_like(jump)
        for k in range(1, teams):
            @pl.when(team + k < teams)
            def _():
                state_copy(k, g).start()
        for k in range(1, teams):
            @pl.when(team >= k)
            def _():
                state_copy(k, g).wait_recv()
                carry[g, 0] += carry[g, k] * jnp.exp(-rates[:, mine] * float((k - 1) * span))
        incoming = carry[g, 0]
        for s in range(SEGS):
            state[g, :, s, :] = state[g, :, s, :] + incoming * jnp.exp(-rate * float(s * seg))

        weight = [row(gains, m) * jnp.sqrt(2.0 * row(rates, m)) for m in range(modes)]
        direct = jnp.broadcast_to(skip[0:1, mine], (SEGS, LANES))

        def second_step(t, states):
            where = pl.ds(pl.multiple_of(t * SEGS, SEGS), SEGS)
            x = prod[g, where, :]
            states = tuple(a * s + x for a, s in zip(keep, states))
            terms = [w * s for w, s in zip(weight, states)] + [direct * x]
            while len(terms) > 1:
                terms = [a + b for a, b in zip(terms[::2], terms[1::2])] + ([terms[-1]] if len(terms) % 2 else [])
            gate[g, where, :] = gate[g, where, :] * terms[0]
            return states

        lax.fori_loop(0, seg, second_step, tuple(state[g, m] for m in range(modes)))

        @pl.loop(0, SEGS)
        def _(s):
            value = gate[g, pl.ds(s, seg, stride=SEGS), :]
            sent[g, pl.ds(pl.multiple_of(s * seg, 8), seg), :] = value.astype(sent.dtype)

    def out_rows(p, g):
        return sent.at[g, pl.ds(pl.multiple_of(p * rows, 16), rows), :]

    def out_copy(d, g):
        peer = flip_traced(place, d, groups)
        return pltpu.make_async_remote_copy(
            src_ref=out_rows(peer, g),
            dst_ref=out.at[:, columns[g]],
            send_sem=out_ssem.at[g, d],
            recv_sem=out_rsem.at[g, d],
            device_id=(team * groups + peer, ch),
            device_id_type=pl.DeviceIdType.MESH,
        )

    def out_arrival(d, g):
        peer = flip_traced(place, d, groups)
        spot = out.at[:, pl.ds(pl.multiple_of(peer * wide + g * LANES, LANES), LANES)]
        return pltpu.make_async_remote_copy(
            src_ref=spot,
            dst_ref=spot,
            send_sem=out_ssem.at[g, d],
            recv_sem=out_rsem.at[g, d],
            device_id=(team * groups + peer, ch),
            device_id_type=pl.DeviceIdType.MESH,
        )

    own_out = [pltpu.make_async_copy(out_rows(place, g), out.at[:, columns[g]], own_sems.at[1, g]) for g in range(lane_groups)]
    for g in range(lane_groups):
        project(g)
        convolve(g)

        @pl.loop(1, groups)
        def _(d):
            out_copy(groups - d, g).start()

        own_out[g].start()

    for i in range(depth):
        tok_copy(0, i).wait_send()
    for mask in masks:
        for i in range(mask.bit_length(), depth):
            tok_copy(mask, i).wait_send()

    for g in range(lane_groups):
        @pl.loop(1, n_ctx)
        def _(m):
            w_copy(m, g).wait_send()

        @pl.when(team < teams - 1)
        def _():
            halo_copy(g).wait_send()

        for k in range(1, teams):
            @pl.when(team + k < teams)
            def _():
                state_copy(k, g).wait_send()

        @pl.loop(1, groups)
        def _(d):
            out_arrival(d, g).wait_recv()
            out_copy(d, g).wait_send()

        own_out[g].wait()


def body(n_ctx, n_ch, tokens, w_in, taps, modes_gain, decay, skip):
    rows, width = tokens.shape
    e_rows, _, channels = w_in.shape
    modes = decay.shape[0]
    groups = min(n_ctx // 2, channels // LANES)
    teams = n_ctx // groups
    wide = channels // groups
    span = groups * rows
    parts = wide // LANES
    depth = (groups * n_ch).bit_length() - 1
    w_send = w_in.transpose(1, 0, 2)
    hbm = pl.BlockSpec(memory_space=pl.ANY)
    dma = pltpu.SemaphoreType.DMA
    f32 = jnp.float32
    return pl.pallas_call(
        functools.partial(kernel, n_ctx, n_ch, groups),
        out_shape=jax.ShapeDtypeStruct((rows, channels), jnp.bfloat16),
        in_specs=[hbm] * 6,
        out_specs=hbm,
        scratch_shapes=[
            pltpu.VMEM((3, 3, wide), f32),
            pltpu.VMEM((modes, wide), f32),
            pltpu.VMEM((modes, wide), f32),
            pltpu.VMEM((1, wide), f32),
            pltpu.VMEM((n_ch * groups, rows, width), tokens.dtype),
            pltpu.VMEM((parts, n_ctx, 3, e_rows, LANES), w_in.dtype),
            pltpu.VMEM((parts, SEGS + span, 3 * LANES), f32),
            pltpu.VMEM((parts, span, LANES), f32),
            pltpu.VMEM((parts, span, LANES), f32),
            pltpu.VMEM((parts, modes, SEGS, LANES), f32),
            pltpu.VMEM((parts, modes, LANES), f32),
            pltpu.VMEM((parts, teams, modes, LANES), f32),
            pltpu.VMEM((parts, span, LANES), jnp.bfloat16),
            pltpu.VMEM((parts, SEGS, 3 * LANES), f32),
            pltpu.VMEM((parts, SEGS, 3 * LANES), f32),
            dma((2**depth, depth)),
            dma((2**depth,)),
            dma((parts, n_ctx)),
            dma((parts, n_ctx)),
            dma((parts, groups)),
            dma((parts, groups)),
            dma((parts, teams)),
            dma((parts, teams)),
            dma((parts, 2)),
            dma((7,)),
            dma((2, parts)),
        ],
        compiler_params=pltpu.CompilerParams(
            collective_id=0, has_side_effects=True, vmem_limit_bytes=60 * 1024 * 1024
        ),
    )(tokens, w_send, taps, modes_gain, decay, skip[None])


def solution(mesh):
    in_specs = (
        P("ctx", "ch"),
        P("ctx", None, "ch"),
        P(None, None, "ch"),
        P(None, "ch"),
        P(None, "ch"),
        P("ch"),
    )
    step = functools.partial(body, mesh.shape["ctx"], mesh.shape["ch"])
    return jax.shard_map(step, mesh=mesh, in_specs=in_specs, out_specs=P("ctx", "ch"), check_vma=False)
```
